512 devices in a mesh: slab: 128 (over z_lo, x, y), orb: 4 (over z_hi, core).
Axes of the slice: x: 4, y: 4, z: 16 (z_hi: 2, z_lo: 8; z = z_hi * 8 + z_lo), core: 2. Of those that a mesh axis runs over, the one named last changes fastest.
Arguments:
- orbitals: float32 [4, 512, 256, 512], P('orb', 'slab'), may hold values from -6 to 6
- potential: float32 [512, 256, 512], P('slab'), may hold values from -1 to 1
- coeffs: float32 [3], replicated, may hold values from 0.4 to 1.2
Outputs:
- density: float32 [512, 256, 512], P('slab', 'orb')
The draws below stay inside these ranges and needn't reach their ends.
All inputs are finite; a program needn't handle non-finite values.
Results may differ from the reference program's by a relative error of at most 0.00002.
Values sent between devices are 32-bit elements; how exact they have to be, the bound alone decides.
A program may use at most 128 MiB of HBM per device.

```python
import jax
import jax.numpy as jnp

NX = 256
NY = 512
TERMS = 3
NZ = 512
ORBS = 4


def levels(key, shape, cuts, smallest, top_value):
    level, own = 1.0, jax.random.fold_in(key, 6)
    for position, parts in cuts:
        steps = jnp.exp(jax.random.uniform(jax.random.fold_in(own, position), (parts,), jnp.float32, smallest / len(cuts), top_value / len(cuts)))
        level = level * jnp.repeat(steps, shape[position] // parts).reshape([-1 if axis == position else 1 for axis in range(len(shape))])
    return level


def centred(key, extent, scale, most, cuts=(), kind=jnp.bfloat16):
    level = levels(key, extent, cuts, -0.22, 0.18) if cuts else 1.0
    drawn = jax.random.normal(key, extent, jnp.float32) * scale * level
    return jnp.minimum(jnp.maximum(drawn, -most), most).astype(kind)


def setup_inputs(seed: int = 0) -> dict:
    streams_of = jax.random.split(jax.random.key(seed), 4)
    orbitals = centred(streams_of[0], (ORBS, NZ, NX, NY), 1.0, 6.0, ((0, 4), (1, 128)), jnp.float32)
    potential = jnp.clip(jax.random.uniform(streams_of[1], (NZ, NX, NY), jnp.float32, -1.0, 1.0) * levels(streams_of[1], (NZ, NX, NY), ((0, 128),), -0.4, 0.0), -1.0, 1.0)
    coeffs = jnp.clip(jax.random.uniform(streams_of[2], (TERMS,), jnp.float32, 0.4, 1.2), 0.4, 1.2)
    return {"orbitals": orbitals, "potential": potential, "coeffs": coeffs}


def laplace(field):
    total = jnp.zeros_like(field)
    for axis in range(3):
        near = jnp.roll(field, 1, axis) + jnp.roll(field, -1, axis)
        far = jnp.roll(field, 2, axis) + jnp.roll(field, -2, axis)
        total = total + (-2.5 * field + (4.0 / 3.0) * near - (1.0 / 12.0) * far)
    return total


def scaled(field, potential):
    return ((-0.5 * laplace(field) + potential * field) - 4.0 * field) / 5.0


def reference(orbitals, potential, coeffs):
    accum = jnp.zeros(potential.shape, jnp.float32)
    for index in range(ORBS):
        psi = orbitals[index]
        first = scaled(psi, potential)
        second = 2.0 * scaled(first, potential) - psi
        filtered = coeffs[0] * psi + coeffs[1] * first + coeffs[2] * second
        accum = accum + filtered * filtered
    return accum / ORBS
```

```python
import jax
import jax.numpy as jnp
from jax import lax
from jax.experimental import pallas as pl
from jax.experimental.pallas import tpu as pltpu
from jax.sharding import PartitionSpec as P

MESH = pl.DeviceIdType.MESH
STEPS = 8
AHEAD = 3


def stencil(cur, prev, nxt, z):
    row = lax.broadcasted_iota(jnp.int32, cur.shape, 0)
    n = cur.shape[1]
    near = pltpu.roll(jnp.where(row == 7, prev, cur), 1, 0) + pltpu.roll(jnp.where(row == 0, nxt, cur), 7, 0)
    far = pltpu.roll(jnp.where(row >= 6, prev, cur), 2, 0) + pltpu.roll(jnp.where(row <= 1, nxt, cur), 6, 0)
    near = near + (pltpu.roll(cur, 1, 1) + pltpu.roll(cur, n - 1, 1)) + (z[1] + z[2])
    far = far + (pltpu.roll(cur, 2, 1) + pltpu.roll(cur, n - 2, 1)) + (z[0] + z[3])
    return far * (1.0 / 120.0) - near * (2.0 / 15.0)


def kernel(
    coef, psi_hbm, pot_hbm, out, psi, pot, first, h1, h2, term, got, zsend, zgot,
    load_sem, s1, r1, s2, r2, cs, cr, zs, zr,
):
    s, o = lax.axis_index("slab"), lax.axis_index("orb")
    count = lax.axis_size("slab")
    core, half = lax.rem(o, 2), o // 2
    up = {"slab": lax.rem(s + 1, count), "orb": o}
    down = {"slab": lax.rem(s + count - 1, count), "orb": o}
    mate = {"slab": s, "orb": o + 1 - 2 * core}
    far_chip = {"slab": s, "orb": lax.rem(o + 2, 4)}

    barrier = pltpu.get_barrier_semaphore()
    for who in (far_chip, up, down, mate):
        pl.semaphore_signal(barrier, inc=1, device_id=who, device_id_type=MESH)
    loads = [
        pltpu.make_async_copy(psi_hbm, psi, load_sem.at[0]),
        pltpu.make_async_copy(pot_hbm, pot, load_sem.at[1]),
    ]
    for copy in loads:
        copy.start()
    pl.semaphore_wait(barrier, 4)

    def halo(src, dst, send, recv, k):
        return [
            pltpu.make_async_remote_copy(
                src_ref=src.at[pl.ds(2, 2), :, k],
                dst_ref=dst.at[0, :, :, k],
                send_sem=send.at[0, k],
                recv_sem=recv.at[0, k],
                device_id=up,
                device_id_type=MESH,
            ),
            pltpu.make_async_remote_copy(
                src_ref=src.at[pl.ds(0, 2), :, k],
                dst_ref=dst.at[1, :, :, k],
                send_sem=send.at[1, k],
                recv_sem=recv.at[1, k],
                device_id=down,
                device_id_type=MESH,
            ),
        ]

    one = [halo(psi_hbm, h1, s1, r1, k) for k in range(STEPS)]
    two = [halo(first, h2, s2, r2, k) for k in range(STEPS)]
    to_mate = [
        pltpu.make_async_remote_copy(
            src_ref=term.at[1 - core, :, :, k],
            dst_ref=got.at[:, :, k],
            send_sem=cs.at[k],
            recv_sem=cr.at[k],
            device_id=mate,
            device_id_type=MESH,
        )
        for k in range(STEPS)
    ]
    to_far = [
        pltpu.make_async_remote_copy(
            src_ref=zsend.at[:, k],
            dst_ref=zgot.at[:, k],
            send_sem=zs.at[k],
            recv_sem=zr.at[k],
            device_id=far_chip,
            device_id_type=MESH,
        )
        for k in range(STEPS)
    ]

    def start(copies):
        for copy in copies:
            copy.start()

    def received(copies):
        for copy in copies:
            copy.wait_recv()

    def tiles(own, halos, j, k):
        flat = j * STEPS + k
        before, after = lax.rem(flat + 31, 32), lax.rem(flat + 1, 32)
        planes = [halos[0, 0, j, k], halos[0, 1, j, k]]
        planes += [own[p, j, k] for p in range(4)]
        planes += [halos[1, 0, j, k], halos[1, 1, j, k]]
        for p in range(4):
            prev = own[p, before // STEPS, lax.rem(before, STEPS)]
            nxt = own[p, after // STEPS, lax.rem(after, STEPS)]
            z = (planes[p], planes[p + 1], planes[p + 3], planes[p + 4])
            yield p, planes[p + 2], stencil(planes[p + 2], prev, nxt, z)

    def first_step(k):
        def body(j, carry):
            for p, cur, rest in tiles(psi, h1, j, k):
                first[p, j, k] = cur * (pot[p, j, k] * 0.2 - 0.05) + rest
            return carry

        lax.fori_loop(0, 4, body, 0)

    a = 0.5 * (coef[0] - coef[2])
    b = 0.5 * coef[1]
    d = coef[2]

    def second_step(k):
        def body(j, carry):
            for p, cur, rest in tiles(first, h2, j, k):
                scaled = cur * (pot[p, j, k] * 0.2 - 0.05) + rest
                value = a * psi[p, j, k] + b * cur + d * scaled
                term[lax.rem(j, 2), j // 2, p, k] = value * value
            return carry

        lax.fori_loop(0, 4, body, 0)
        to_mate[k].start()

    def far_step(k):
        to_mate[k].wait_recv()
        for p in range(4):
            zsend[p, k] = term[core, 1 - half, p, k] + got[1 - half, p, k]
        to_far[k].start()

    def last_step(k):
        to_far[k].wait_recv()
        for p in range(4):
            out[p, k] = (term[core, half, p, k] + got[half, p, k]) + zgot[p, k]

    for k in range(AHEAD):
        start(one[k])
    for copy in loads:
        copy.wait()
    order = [*range(1, STEPS), 0]
    for k in range(STEPS):
        received(one[k])
        first_step(k)
        if k >= 1:
            start(two[k])
        if k + AHEAD < STEPS:
            start(one[k + AHEAD])
        if k == STEPS - 1:
            start(two[0])
        if k >= 3:
            far_step(k - 2)
        if k >= 2:
            received(two[k - 1])
            second_step(k - 1)
    far_step(STEPS - 2)
    received(two[STEPS - 1])
    second_step(STEPS - 1)
    far_step(STEPS - 1)
    received(two[0])
    second_step(0)
    far_step(0)
    for k in order:
        last_step(k)
    for k in range(STEPS):
        for copy in (*one[k], *two[k], to_mate[k], to_far[k]):
            copy.wait_send()


def shards(orbitals, potential, coeffs):
    planes, rows, width = potential.shape
    grid = (planes, 4, STEPS, rows // (4 * STEPS), width)
    tile = grid[3:]
    halos = pltpu.VMEM((2, 2, 4, STEPS, *tile), jnp.float32)
    whole = pltpu.VMEM(grid, jnp.float32)
    quarter = (planes, STEPS, *tile)
    dma = pltpu.SemaphoreType.DMA
    out = pl.pallas_call(
        kernel,
        out_shape=jax.ShapeDtypeStruct(quarter, jnp.float32),
        in_specs=[
            pl.BlockSpec(memory_space=pltpu.SMEM),
            pl.BlockSpec(memory_space=pl.ANY),
            pl.BlockSpec(memory_space=pl.ANY),
        ],
        out_specs=pl.BlockSpec(memory_space=pltpu.VMEM),
        scratch_shapes=[
            whole, whole, whole, halos, halos,
            pltpu.VMEM((2, 2, *quarter), jnp.float32),
            pltpu.VMEM((2, *quarter), jnp.float32),
            pltpu.VMEM(quarter, jnp.float32),
            pltpu.VMEM(quarter, jnp.float32),
            dma((2,)),
            dma((2, STEPS)), dma((2, STEPS)), dma((2, STEPS)), dma((2, STEPS)),
            dma((STEPS,)), dma((STEPS,)), dma((STEPS,)), dma((STEPS,)),
        ],
        compiler_params=pltpu.CompilerParams(collective_id=0, has_side_effects=True),
        name="filter_density",
    )(coeffs, orbitals.reshape(grid), potential.reshape(grid))
    return out.reshape(planes, rows // 4, width)


def solution(mesh):
    return jax.shard_map(
        shards,
        mesh=mesh,
        in_specs=(P("orb", "slab", None, None), P("slab", None, None), P()),
        out_specs=P("slab", "orb", None),
        check_vma=False,
    )
```

```python
import jax
import jax.numpy as jnp
from jax import lax
from jax.experimental import pallas as pl
from jax.experimental.pallas import tpu as pltpu
from jax.sharding import PartitionSpec as P

MESH = pl.DeviceIdType.MESH
STEPS = 8
AHEAD = 3


def stencil(cur, prev, nxt, z):
    row = lax.broadcasted_iota(jnp.int32, cur.shape, 0)
    n = cur.shape[1]
    near = pltpu.roll(jnp.where(row == 7, prev, cur), 1, 0) + pltpu.roll(jnp.where(row == 0, nxt, cur), 7, 0)
    far = pltpu.roll(jnp.where(row >= 6, prev, cur), 2, 0) + pltpu.roll(jnp.where(row <= 1, nxt, cur), 6, 0)
    near = near + (pltpu.roll(cur, 1, 1) + pltpu.roll(cur, n - 1, 1)) + (z[1] + z[2])
    far = far + (pltpu.roll(cur, 2, 1) + pltpu.roll(cur, n - 2, 1)) + (z[0] + z[3])
    return far * (1.0 / 120.0) - near * (2.0 / 15.0)


def kernel(
    coef, psi_hbm, pot_hbm, out, psi, pot, first, h1, h2, term, got, zsend, zgot, passing,
    load_sem, s1, r1, s2, r2, cs, cr, zs, zr, pass_in, pass_out,
):
    s, o = lax.axis_index("slab"), lax.axis_index("orb")
    count = lax.axis_size("slab")
    core, half = lax.rem(o, 2), o // 2
    up = {"slab": lax.rem(s + 1, count), "orb": o}
    down = {"slab": lax.rem(s + count - 1, count), "orb": o}
    mate = {"slab": s, "orb": o + 1 - 2 * core}
    far_chip = {"slab": s, "orb": lax.rem(o + 2, 4)}

    xy = lax.rem(s, 16)
    group = xy // 8
    turn = xy + group * (15 - 2 * xy)
    edge = s - xy + 15 * group

    def by(k, half_of=None):
        return {"slab": s - xy + k + group * (15 - 2 * k), "orb": o if half_of is None else half_of}

    barrier = pltpu.get_barrier_semaphore()

    @pl.when(turn == 0)
    def _():
        for k in range(1, STEPS):
            pl.semaphore_signal(barrier, inc=1, device_id=by(k, lax.rem(o + 2, 4)), device_id_type=MESH)

    @pl.when(turn != 0)
    def _():
        pl.semaphore_signal(barrier, inc=1, device_id={"slab": edge, "orb": o}, device_id_type=MESH)

    for who in (far_chip, up, down, mate):
        pl.semaphore_signal(barrier, inc=1, device_id=who, device_id_type=MESH)
    loads = [
        pltpu.make_async_copy(psi_hbm, psi, load_sem.at[0]),
        pltpu.make_async_copy(pot_hbm, pot, load_sem.at[1]),
    ]
    for copy in loads:
        copy.start()

    @pl.when(turn == 0)
    def _():
        pl.semaphore_wait(barrier, 4 + STEPS - 1)

    @pl.when(turn != 0)
    def _():
        pl.semaphore_wait(barrier, 5)

    def halo(src, dst, send, recv, k):
        return [
            pltpu.make_async_remote_copy(
                src_ref=src.at[pl.ds(2, 2), :, k],
                dst_ref=dst.at[0, :, :, k],
                send_sem=send.at[0, k],
                recv_sem=recv.at[0, k],
                device_id=up,
                device_id_type=MESH,
            ),
            pltpu.make_async_remote_copy(
                src_ref=src.at[pl.ds(0, 2), :, k],
                dst_ref=dst.at[1, :, :, k],
                send_sem=send.at[1, k],
                recv_sem=recv.at[1, k],
                device_id=down,
                device_id_type=MESH,
            ),
        ]

    one = [halo(psi_hbm, h1, s1, r1, k) for k in range(STEPS)]
    two = [halo(first, h2, s2, r2, k) for k in range(STEPS)]
    to_mate = [
        pltpu.make_async_remote_copy(
            src_ref=term.at[1 - core, :, :, k],
            dst_ref=got.at[:, :, k],
            send_sem=cs.at[k],
            recv_sem=cr.at[k],
            device_id=mate,
            device_id_type=MESH,
        )
        for k in range(STEPS)
    ]
    to_far = [
        pltpu.make_async_remote_copy(
            src_ref=zsend.at[:, k],
            dst_ref=zgot.at[:, k],
            send_sem=zs.at[k],
            recv_sem=zr.at[k],
            device_id=far_chip,
            device_id_type=MESH,
        )
        for k in range(STEPS)
    ]

    to_pass = [
        pltpu.make_async_remote_copy(
            src_ref=zsend.at[:, k],
            dst_ref=passing,
            send_sem=zs.at[k],
            recv_sem=pass_in.at[0],
            device_id=by(k),
            device_id_type=MESH,
        )
        for k in range(STEPS)
    ]

    def start(copies):
        for copy in copies:
            copy.start()

    def received(copies):
        for copy in copies:
            copy.wait_recv()

    def tiles(own, halos, j, k):
        flat = j * STEPS + k
        before, after = lax.rem(flat + 31, 32), lax.rem(flat + 1, 32)
        planes = [halos[0, 0, j, k], halos[0, 1, j, k]]
        planes += [own[p, j, k] for p in range(4)]
        planes += [halos[1, 0, j, k], halos[1, 1, j, k]]
        for p in range(4):
            prev = own[p, before // STEPS, lax.rem(before, STEPS)]
            nxt = own[p, after // STEPS, lax.rem(after, STEPS)]
            z = (planes[p], planes[p + 1], planes[p + 3], planes[p + 4])
            yield p, planes[p + 2], stencil(planes[p + 2], prev, nxt, z)

    def first_step(k):
        def body(j, carry):
            for p, cur, rest in tiles(psi, h1, j, k):
                first[p, j, k] = cur * (pot[p, j, k] * 0.2 - 0.05) + rest
            return carry

        lax.fori_loop(0, 4, body, 0)

    a = 0.5 * (coef[0] - coef[2])
    b = 0.5 * coef[1]
    d = coef[2]

    def second_step(k):
        def body(j, carry):
            for p, cur, rest in tiles(first, h2, j, k):
                scaled = cur * (pot[p, j, k] * 0.2 - 0.05) + rest
                value = a * psi[p, j, k] + b * cur + d * scaled
                term[lax.rem(j, 2), j // 2, p, k] = value * value
            return carry

        lax.fori_loop(0, 4, body, 0)
        to_mate[k].start()

    def far_step(k):
        to_mate[k].wait_recv()
        for p in range(4):
            zsend[p, k] = term[core, 1 - half, p, k] + got[1 - half, p, k]
        if k == 0:
            to_far[k].start()
        else:
            pl.when(turn == 0)(to_pass[k].start)
            pl.when(turn != 0)(to_far[k].start)

    def pass_on(k):
        @pl.when(turn == k)
        def _():
            to_pass[k].wait_recv()
            copy = pltpu.make_async_remote_copy(
                src_ref=passing,
                dst_ref=zgot.at[:, k],
                send_sem=pass_out.at[0],
                recv_sem=zr.at[k],
                device_id={"slab": edge, "orb": lax.rem(o + 2, 4)},
                device_id_type=MESH,
            )
            copy.start()
            copy.wait_send()

    def last_step(k):
        to_far[k].wait_recv()
        for p in range(4):
            out[p, k] = (term[core, half, p, k] + got[half, p, k]) + zgot[p, k]

    for k in range(AHEAD):
        start(one[k])
    for copy in loads:
        copy.wait()
    order = [*range(1, STEPS), 0]
    for k in range(STEPS):
        received(one[k])
        first_step(k)
        if k >= 1:
            start(two[k])
        if k + AHEAD < STEPS:
            start(one[k + AHEAD])
        if k == STEPS - 1:
            start(two[0])
        if k >= 3:
            far_step(k - 2)
        if k >= 2:
            received(two[k - 1])
            second_step(k - 1)
        if k >= STEPS - 2:
            pass_on(k - STEPS + 3)
    far_step(STEPS - 2)
    received(two[STEPS - 1])
    second_step(STEPS - 1)
    far_step(STEPS - 1)
    received(two[0])
    second_step(0)
    far_step(0)
    for k in range(3, STEPS):
        pass_on(k)
    for k in order:
        last_step(k)
    for k in range(STEPS):
        for copy in (*one[k], *two[k], to_mate[k], to_far[k]):
            copy.wait_send()


def shards(orbitals, potential, coeffs):
    planes, rows, width = potential.shape
    grid = (planes, 4, STEPS, rows // (4 * STEPS), width)
    tile = grid[3:]
    halos = pltpu.VMEM((2, 2, 4, STEPS, *tile), jnp.float32)
    whole = pltpu.VMEM(grid, jnp.float32)
    quarter = (planes, STEPS, *tile)
    dma = pltpu.SemaphoreType.DMA
    out = pl.pallas_call(
        kernel,
        out_shape=jax.ShapeDtypeStruct(quarter, jnp.float32),
        in_specs=[
            pl.BlockSpec(memory_space=pltpu.SMEM),
            pl.BlockSpec(memory_space=pl.ANY),
            pl.BlockSpec(memory_space=pl.ANY),
        ],
        out_specs=pl.BlockSpec(memory_space=pltpu.VMEM),
        scratch_shapes=[
            whole, whole, whole, halos, halos,
            pltpu.VMEM((2, 2, *quarter), jnp.float32),
            pltpu.VMEM((2, *quarter), jnp.float32),
            pltpu.VMEM(quarter, jnp.float32),
            pltpu.VMEM(quarter, jnp.float32),
            pltpu.VMEM((planes, *tile), jnp.float32),
            dma((2,)),
            dma((2, STEPS)), dma((2, STEPS)), dma((2, STEPS)), dma((2, STEPS)),
            dma((STEPS,)), dma((STEPS,)), dma((STEPS,)), dma((STEPS,)), dma((1,)), dma((1,)),
        ],
        compiler_params=pltpu.CompilerParams(collective_id=0, has_side_effects=True),
        name="filter_density",
    )(coeffs, orbitals.reshape(grid), potential.reshape(grid))
    return out.reshape(planes, rows // 4, width)


def solution(mesh):
    return jax.shard_map(
        shards,
        mesh=mesh,
        in_specs=(P("orb", "slab", None, None), P("slab", None, None), P()),
        out_specs=P("slab", "orb", None),
        check_vma=False,
    )
```

```python
import jax
import jax.numpy as jnp
from jax import lax
from jax.experimental import pallas as pl
from jax.experimental.pallas import tpu as pltpu
from jax.sharding import PartitionSpec as P

MESH = pl.DeviceIdType.MESH
STEPS = 16
TURNS = STEPS // 2
AHEAD, AHEAD_TURN, AHEAD_WRAP = 4, 4, 10
LAG, LAG_TURN, LAG_WRAP = 1, 1, 4
PASS = 8


def stencil(cur, prev, nxt, z):
    row = lax.broadcasted_iota(jnp.int32, cur.shape, 0)
    n = cur.shape[1]
    near = pltpu.roll(jnp.where(row == 7, prev, cur), 1, 0) + pltpu.roll(jnp.where(row == 0, nxt, cur), 7, 0)
    far = pltpu.roll(jnp.where(row >= 6, prev, cur), 2, 0) + pltpu.roll(jnp.where(row <= 1, nxt, cur), 6, 0)
    near = near + (pltpu.roll(cur, 1, 1) + pltpu.roll(cur, n - 1, 1)) + (z[1] + z[2])
    far = far + (pltpu.roll(cur, 2, 1) + pltpu.roll(cur, n - 2, 1)) + (z[0] + z[3])
    return far * (1.0 / 120.0) - near * (2.0 / 15.0)


def kernel(
    coef, psi_hbm, pot_hbm, out, psi, pot, first, h1, h2, term, got, zsend, zgot, passing,
    load_sem, s1, r1, s2, r2, cs, cr, zs, zr, pass_in, pass_out,
):
    s, o = lax.axis_index("slab"), lax.axis_index("orb")
    count = lax.axis_size("slab")
    core, half = lax.rem(o, 2), o // 2
    up = {"slab": lax.rem(s + 1, count), "orb": o}
    down = {"slab": lax.rem(s + count - 1, count), "orb": o}
    mate = {"slab": s, "orb": o + 1 - 2 * core}
    far_chip = {"slab": s, "orb": lax.rem(o + 2, 4)}

    xy = lax.rem(s, 16)
    group = xy // 8
    turn = xy + group * (15 - 2 * xy)
    edge = s - xy + 15 * group

    def by(k, half_of=None):
        return {"slab": s - xy + k + group * (15 - 2 * k), "orb": o if half_of is None else half_of}

    barrier = pltpu.get_barrier_semaphore()

    @pl.when(turn == 0)
    def _():
        for k in range(1, TURNS):
            pl.semaphore_signal(barrier, inc=1, device_id=by(k, lax.rem(o + 2, 4)), device_id_type=MESH)

    @pl.when(turn != 0)
    def _():
        pl.semaphore_signal(barrier, inc=1, device_id={"slab": edge, "orb": o}, device_id_type=MESH)

    for who in (far_chip, up, down, mate):
        pl.semaphore_signal(barrier, inc=1, device_id=who, device_id_type=MESH)
    loads = [
        pltpu.make_async_copy(psi_hbm, psi, load_sem.at[0]),
        pltpu.make_async_copy(pot_hbm, pot, load_sem.at[1]),
    ]
    for copy in loads:
        copy.start()

    @pl.when(turn == 0)
    def _():
        pl.semaphore_wait(barrier, 4 + TURNS - 1)

    @pl.when(turn != 0)
    def _():
        pl.semaphore_wait(barrier, 5)

    def halo(src, dst, send, recv, k):
        return [
            pltpu.make_async_remote_copy(
                src_ref=src.at[pl.ds(2, 2), :, k],
                dst_ref=dst.at[0, :, :, k],
                send_sem=send.at[0, k],
                recv_sem=recv.at[0, k],
                device_id=up,
                device_id_type=MESH,
            ),
            pltpu.make_async_remote_copy(
                src_ref=src.at[pl.ds(0, 2), :, k],
                dst_ref=dst.at[1, :, :, k],
                send_sem=send.at[1, k],
                recv_sem=recv.at[1, k],
                device_id=down,
                device_id_type=MESH,
            ),
        ]

    def one(k):
        return halo(psi_hbm, h1, s1, r1, k)

    def two(k):
        return halo(first, h2, s2, r2, k)

    def to_mate(r):
        return pltpu.make_async_remote_copy(
            src_ref=term.at[1 - core, :, :, r],
            dst_ref=got.at[:, :, r],
            send_sem=cs.at[r],
            recv_sem=cr.at[r],
            device_id=mate,
            device_id_type=MESH,
        )

    def to_far(r):
        return pltpu.make_async_remote_copy(
            src_ref=zsend.at[:, r],
            dst_ref=zgot.at[:, r],
            send_sem=zs.at[r],
            recv_sem=zr.at[r],
            device_id=far_chip,
            device_id_type=MESH,
        )

    def to_pass(r, column):
        return pltpu.make_async_remote_copy(
            src_ref=zsend.at[:, r],
            dst_ref=passing,
            send_sem=zs.at[r],
            recv_sem=pass_in.at[0],
            device_id=by(column),
            device_id_type=MESH,
        )

    def start(copies):
        for copy in copies:
            copy.start()

    def received(copies):
        for copy in copies:
            copy.wait_recv()

    def tiles(own, halos, j, k):
        flat = j * STEPS + k
        before, after = lax.rem(flat + 2 * STEPS - 1, 2 * STEPS), lax.rem(flat + 1, 2 * STEPS)
        planes = [halos[0, 0, j, k], halos[0, 1, j, k]]
        planes += [own[p, j, k] for p in range(4)]
        planes += [halos[1, 0, j, k], halos[1, 1, j, k]]
        for p in range(4):
            prev = own[p, before // STEPS, lax.rem(before, STEPS)]
            nxt = own[p, after // STEPS, lax.rem(after, STEPS)]
            z = (planes[p], planes[p + 1], planes[p + 3], planes[p + 4])
            yield p, planes[p + 2], stencil(planes[p + 2], prev, nxt, z)

    def first_step(k):
        def body(j, carry):
            for p, cur, rest in tiles(psi, h1, j, k):
                first[p, j, k] = cur * (pot[p, j, k] * 0.2 - 0.05) + rest
            return carry

        lax.fori_loop(0, 2, body, 0)

    a = 0.5 * (coef[0] - coef[2])
    b = 0.5 * coef[1]
    d = coef[2]

    def second_step(k):
        owner, r = k // TURNS, lax.rem(k, TURNS)

        def body(j, carry):
            for p, cur, rest in tiles(first, h2, j, k):
                scaled = cur * (pot[p, j, k] * 0.2 - 0.05) + rest
                value = a * psi[p, j, k] + b * cur + d * scaled
                term[owner, j, p, r] = value * value
            return carry

        lax.fori_loop(0, 2, body, 0)

        @pl.when(core != owner)
        def _():
            to_mate(r).start()

    def far_step(k):
        owner, r = k // TURNS, lax.rem(k, TURNS)

        @pl.when(core == owner)
        def _():
            to_mate(r).wait_recv()
            for p in range(4):
                zsend[p, r] = term[owner, 1 - half, p, r] + got[1 - half, p, r]
            column = lax.rem(r + core, TURNS)
            passes = jnp.logical_and(turn == 0, column != 0)

            @pl.when(passes)
            def _():
                to_pass(r, column).start()

            @pl.when(jnp.logical_not(passes))
            def _():
                to_far(r).start()

    def pass_on():
        to_pass(pass_row, turn).wait_recv()
        copy = pltpu.make_async_remote_copy(
            src_ref=passing,
            dst_ref=zgot.at[:, pass_row],
            send_sem=pass_out.at[0],
            recv_sem=zr.at[pass_row],
            device_id={"slab": edge, "orb": lax.rem(o + 2, 4)},
            device_id_type=MESH,
        )
        copy.start()
        copy.wait_send()

    def each(first_k, last_k, body):
        def step(k, carry):
            body(k)
            return carry

        lax.fori_loop(first_k, last_k, step, 0)

    def wraps(slab, width):
        return lax.rem(slab + width, count) // (2 * width) == 0

    turns = lax.rem(s + 1, 4) // 2 == 0
    ahead = jnp.where(wraps(s, 1), AHEAD_WRAP, jnp.where(turns, AHEAD_TURN, AHEAD))
    lag = jnp.where(wraps(s, 2), LAG_WRAP, jnp.where(turns, LAG_TURN, LAG))
    pass_row = lax.rem(turn - core + TURNS, TURNS)
    pass_slot = core * TURNS + pass_row + jnp.where(wraps(edge, 1), LAG_WRAP, LAG_TURN) + PASS

    each(0, ahead, lambda k: start(one(k)))
    for copy in loads:
        copy.wait()

    def slot(t):
        @pl.when(t < STEPS)
        def _():
            received(one(t))
            first_step(t)

            @pl.when(t > 0)
            def _():
                start(two(t))

            @pl.when(t + ahead < STEPS)
            def _():
                start(one(t + ahead))

            @pl.when(t == STEPS - 1)
            def _():
                start(two(0))

        m = t - lag

        @pl.when(jnp.logical_and(m > 1, m < STEPS + 2))
        def _():
            far_step(lax.rem(m - 1, STEPS))

        @pl.when(jnp.logical_and(m > 0, m < STEPS + 1))
        def _():
            k = lax.rem(m, STEPS)
            received(two(k))
            second_step(k)

        @pl.when(jnp.logical_and(t == pass_slot, turn != 0))
        def _():
            pass_on()

    each(0, STEPS + 2 + LAG_WRAP + PASS, slot)

    def last_step(r):
        to_far(r).wait_recv()
        for p in range(4):
            out[p, r] = (term[core, half, p, r] + got[half, p, r]) + zgot[p, r]

    each(0, TURNS, last_step)

    def sent(k):
        for copy in (*one(k), *two(k)):
            copy.wait_send()

    each(0, STEPS, sent)

    def sums_sent(r):
        to_mate(r).wait_send()
        to_far(r).wait_send()

    each(0, TURNS, sums_sent)


def shards(orbitals, potential, coeffs):
    planes, rows, width = potential.shape
    grid = (planes, 2, STEPS, rows // (2 * STEPS), width)
    tile = grid[3:]
    halos = pltpu.VMEM((2, 2, 2, STEPS, *tile), jnp.float32)
    whole = pltpu.VMEM(grid, jnp.float32)
    quarter = (planes, TURNS, *tile)
    dma = pltpu.SemaphoreType.DMA
    out = pl.pallas_call(
        kernel,
        out_shape=jax.ShapeDtypeStruct(quarter, jnp.float32),
        in_specs=[
            pl.BlockSpec(memory_space=pltpu.SMEM),
            pl.BlockSpec(memory_space=pl.ANY),
            pl.BlockSpec(memory_space=pl.ANY),
        ],
        out_specs=pl.BlockSpec(memory_space=pltpu.VMEM),
        scratch_shapes=[
            whole, whole, whole, halos, halos,
            pltpu.VMEM((2, 2, *quarter), jnp.float32),
            pltpu.VMEM((2, *quarter), jnp.float32),
            pltpu.VMEM(quarter, jnp.float32),
            pltpu.VMEM(quarter, jnp.float32),
            pltpu.VMEM((planes, *tile), jnp.float32),
            dma((2,)),
            dma((2, STEPS)), dma((2, STEPS)), dma((2, STEPS)), dma((2, STEPS)),
            dma((TURNS,)), dma((TURNS,)), dma((TURNS,)), dma((TURNS,)), dma((1,)), dma((1,)),
        ],
        compiler_params=pltpu.CompilerParams(collective_id=0, has_side_effects=True),
        name="filter_density",
    )(coeffs, orbitals.reshape(grid), potential.reshape(grid))
    return out.reshape(planes, rows // 4, width)


def solution(mesh):
    return jax.shard_map(
        shards,
        mesh=mesh,
        in_specs=(P("orb", "slab", None, None), P("slab", None, None), P()),
        out_specs=P("slab", "orb", None),
        check_vma=False,
    )
```

```python
import jax
import jax.numpy as jnp
from jax import lax
from jax.experimental import pallas as pl
from jax.experimental.pallas import tpu as pltpu
from jax.sharding import PartitionSpec as P

MESH = pl.DeviceIdType.MESH
STEPS = 16
TURNS = STEPS // 2
AHEAD = (4, 4, 5, 5, 10)
LAG = (1, 1, 2, 4, 4)
DIRECT = 2
PASS = 8


def stencil(cur, prev, nxt, z):
    row = lax.broadcasted_iota(jnp.int32, cur.shape, 0)
    n = cur.shape[1]
    near = pltpu.roll(jnp.where(row == 7, prev, cur), 1, 0) + pltpu.roll(jnp.where(row == 0, nxt, cur), 7, 0)
    far = pltpu.roll(jnp.where(row >= 6, prev, cur), 2, 0) + pltpu.roll(jnp.where(row <= 1, nxt, cur), 6, 0)
    near = near + (pltpu.roll(cur, 1, 1) + pltpu.roll(cur, n - 1, 1)) + (z[1] + z[2])
    far = far + (pltpu.roll(cur, 2, 1) + pltpu.roll(cur, n - 2, 1)) + (z[0] + z[3])
    return far * (1.0 / 120.0) - near * (2.0 / 15.0)


def kernel(
    coef, psi_hbm, pot_hbm, out, psi, pot, first, h1, h2, term, got, zsend, zgot, passing,
    load_sem, s1, r1, s2, r2, cs, cr, zs, zr, pass_in, pass_out,
):
    s, o = lax.axis_index("slab"), lax.axis_index("orb")
    count = lax.axis_size("slab")
    core, half = lax.rem(o, 2), o // 2
    up = {"slab": lax.rem(s + 1, count), "orb": o}
    down = {"slab": lax.rem(s + count - 1, count), "orb": o}
    mate = {"slab": s, "orb": o + 1 - 2 * core}
    far_chip = {"slab": s, "orb": lax.rem(o + 2, 4)}

    xy = lax.rem(s, 16)
    group = xy // 8
    turn = xy + group * (15 - 2 * xy)
    edge = s - xy + 15 * group

    def by(k, half_of=None):
        return {"slab": s - xy + k + group * (15 - 2 * k), "orb": o if half_of is None else half_of}

    barrier = pltpu.get_barrier_semaphore()

    @pl.when(turn == 0)
    def _():
        for k in range(1, TURNS):
            pl.semaphore_signal(barrier, inc=1, device_id=by(k, lax.rem(o + 2, 4)), device_id_type=MESH)

    @pl.when(turn != 0)
    def _():
        pl.semaphore_signal(barrier, inc=1, device_id={"slab": edge, "orb": o}, device_id_type=MESH)

    for who in (far_chip, up, down, mate):
        pl.semaphore_signal(barrier, inc=1, device_id=who, device_id_type=MESH)
    loads = [
        pltpu.make_async_copy(psi_hbm, psi, load_sem.at[0]),
        pltpu.make_async_copy(pot_hbm, pot, load_sem.at[1]),
    ]
    for copy in loads:
        copy.start()

    @pl.when(turn == 0)
    def _():
        pl.semaphore_wait(barrier, 4 + TURNS - 1)

    @pl.when(turn != 0)
    def _():
        pl.semaphore_wait(barrier, 5)

    def halo(src, dst, send, recv, k):
        return [
            pltpu.make_async_remote_copy(
                src_ref=src.at[pl.ds(2, 2), :, k],
                dst_ref=dst.at[0, :, :, k],
                send_sem=send.at[0, k],
                recv_sem=recv.at[0, k],
                device_id=up,
                device_id_type=MESH,
            ),
            pltpu.make_async_remote_copy(
                src_ref=src.at[pl.ds(0, 2), :, k],
                dst_ref=dst.at[1, :, :, k],
                send_sem=send.at[1, k],
                recv_sem=recv.at[1, k],
                device_id=down,
                device_id_type=MESH,
            ),
        ]

    def one(k):
        return halo(psi_hbm, h1, s1, r1, STEPS - 1 - k)

    def two(k):
        return halo(first, h2, s2, r2, STEPS - 1 - k)

    def to_mate(r):
        return pltpu.make_async_remote_copy(
            src_ref=term.at[1 - core, :, :, r],
            dst_ref=got.at[:, :, r],
            send_sem=cs.at[r],
            recv_sem=cr.at[r],
            device_id=mate,
            device_id_type=MESH,
        )

    def to_far(r):
        return pltpu.make_async_remote_copy(
            src_ref=zsend.at[:, r],
            dst_ref=zgot.at[:, r],
            send_sem=zs.at[r],
            recv_sem=zr.at[r],
            device_id=far_chip,
            device_id_type=MESH,
        )

    def to_pass(r, column):
        return pltpu.make_async_remote_copy(
            src_ref=zsend.at[:, r],
            dst_ref=passing,
            send_sem=zs.at[r],
            recv_sem=pass_in.at[0],
            device_id=by(column),
            device_id_type=MESH,
        )

    def start(copies):
        for copy in copies:
            copy.start()

    def received(copies):
        for copy in copies:
            copy.wait_recv()

    def tiles(own, halos, j, k):
        flat = j * STEPS + k
        before, after = lax.rem(flat + 2 * STEPS - 1, 2 * STEPS), lax.rem(flat + 1, 2 * STEPS)
        planes = [halos[0, 0, j, k], halos[0, 1, j, k]]
        planes += [own[p, j, k] for p in range(4)]
        planes += [halos[1, 0, j, k], halos[1, 1, j, k]]
        for p in range(4):
            prev = own[p, before // STEPS, lax.rem(before, STEPS)]
            nxt = own[p, after // STEPS, lax.rem(after, STEPS)]
            z = (planes[p], planes[p + 1], planes[p + 3], planes[p + 4])
            yield p, planes[p + 2], stencil(planes[p + 2], prev, nxt, z)

    def first_step(step):
        k = STEPS - 1 - step

        def body(j, carry):
            for p, cur, rest in tiles(psi, h1, j, k):
                first[p, j, k] = cur * (pot[p, j, k] * 0.2 - 0.05) + rest
            return carry

        lax.fori_loop(0, 2, body, 0)

    a = 0.5 * (coef[0] - coef[2])
    b = 0.5 * coef[1]
    d = coef[2]

    def second_step(step):
        k = STEPS - 1 - step
        owner, r = k // TURNS, lax.rem(k, TURNS)

        def body(j, carry):
            for p, cur, rest in tiles(first, h2, j, k):
                scaled = cur * (pot[p, j, k] * 0.2 - 0.05) + rest
                value = a * psi[p, j, k] + b * cur + d * scaled
                term[owner, j, p, r] = value * value
            return carry

        lax.fori_loop(0, 2, body, 0)

        @pl.when(core != owner)
        def _():
            to_mate(r).start()

    def far_step(step):
        k = STEPS - 1 - step
        owner, r = k // TURNS, lax.rem(k, TURNS)

        @pl.when(core == owner)
        def _():
            to_mate(r).wait_recv()
            for p in range(4):
                zsend[p, r] = term[owner, 1 - half, p, r] + got[1 - half, p, r]
            column = lax.rem(r + core, TURNS)
            passes = jnp.logical_and(turn == 0, column >= DIRECT)

            @pl.when(passes)
            def _():
                to_pass(r, column).start()

            @pl.when(jnp.logical_not(passes))
            def _():
                to_far(r).start()

    def pass_on():
        to_pass(pass_row, turn).wait_recv()
        copy = pltpu.make_async_remote_copy(
            src_ref=passing,
            dst_ref=zgot.at[:, pass_row],
            send_sem=pass_out.at[0],
            recv_sem=zr.at[pass_row],
            device_id={"slab": edge, "orb": lax.rem(o + 2, 4)},
            device_id_type=MESH,
        )
        copy.start()
        copy.wait_send()

    def each(first_k, last_k, body):
        def step(k, carry):
            body(k)
            return carry

        lax.fori_loop(first_k, last_k, step, 0)

    def wraps(slab, width):
        return lax.rem(slab + width, count) // (2 * width) == 0

    def pick(table, slab):
        value = jnp.where(lax.rem(slab + 1, 4) // 2 == 0, table[1], table[0])
        value = jnp.where(lax.rem(slab + 1, 16) // 2 == 0, table[2], value)
        value = jnp.where(wraps(slab, 2), table[3], value)
        return jnp.where(wraps(slab, 1), table[4], value)

    ahead, lag = pick(AHEAD, s), pick(LAG, s)
    pass_row = lax.rem(turn - core + TURNS, TURNS)
    pass_slot = STEPS - 1 - core * TURNS - pass_row + pick(LAG, edge) + PASS

    each(0, ahead, lambda k: start(one(k)))
    for copy in loads:
        copy.wait()

    def slot(t):
        @pl.when(t < STEPS)
        def _():
            received(one(t))
            first_step(t)

            @pl.when(t > 0)
            def _():
                start(two(t))

            @pl.when(t + ahead < STEPS)
            def _():
                start(one(t + ahead))

            @pl.when(t == STEPS - 1)
            def _():
                start(two(0))

        m = t - lag

        @pl.when(jnp.logical_and(m > 1, m < STEPS + 2))
        def _():
            far_step(lax.rem(m - 1, STEPS))

        @pl.when(jnp.logical_and(m > 0, m < STEPS + 1))
        def _():
            k = lax.rem(m, STEPS)
            received(two(k))
            second_step(k)

        @pl.when(jnp.logical_and(t == pass_slot, turn >= DIRECT))
        def _():
            pass_on()

    each(0, STEPS + 2 + max(LAG) + PASS, slot)

    def last_step(r):
        to_far(r).wait_recv()
        for p in range(4):
            out[p, r] = (term[core, half, p, r] + got[half, p, r]) + zgot[p, r]

    each(0, TURNS, last_step)

    def sent(k):
        for copy in (*one(k), *two(k)):
            copy.wait_send()

    each(0, STEPS, sent)

    def sums_sent(r):
        to_mate(r).wait_send()
        to_far(r).wait_send()

    each(0, TURNS, sums_sent)


def shards(orbitals, potential, coeffs):
    planes, rows, width = potential.shape
    grid = (planes, 2, STEPS, rows // (2 * STEPS), width)
    tile = grid[3:]
    halos = pltpu.VMEM((2, 2, 2, STEPS, *tile), jnp.float32)
    whole = pltpu.VMEM(grid, jnp.float32)
    quarter = (planes, TURNS, *tile)
    dma = pltpu.SemaphoreType.DMA
    out = pl.pallas_call(
        kernel,
        out_shape=jax.ShapeDtypeStruct(quarter, jnp.float32),
        in_specs=[
            pl.BlockSpec(memory_space=pltpu.SMEM),
            pl.BlockSpec(memory_space=pl.ANY),
            pl.BlockSpec(memory_space=pl.ANY),
        ],
        out_specs=pl.BlockSpec(memory_space=pltpu.VMEM),
        scratch_shapes=[
            whole, whole, whole, halos, halos,
            pltpu.VMEM((2, 2, *quarter), jnp.float32),
            pltpu.VMEM((2, *quarter), jnp.float32),
            pltpu.VMEM(quarter, jnp.float32),
            pltpu.VMEM(quarter, jnp.float32),
            pltpu.VMEM((planes, *tile), jnp.float32),
            dma((2,)),
            dma((2, STEPS)), dma((2, STEPS)), dma((2, STEPS)), dma((2, STEPS)),
            dma((TURNS,)), dma((TURNS,)), dma((TURNS,)), dma((TURNS,)), dma((1,)), dma((1,)),
        ],
        compiler_params=pltpu.CompilerParams(collective_id=0, has_side_effects=True),
        name="filter_density",
    )(coeffs, orbitals.reshape(grid), potential.reshape(grid))
    return out.reshape(planes, rows // 4, width)


def solution(mesh):
    return jax.shard_map(
        shards,
        mesh=mesh,
        in_specs=(P("orb", "slab", None, None), P("slab", None, None), P()),
        out_specs=P("slab", "orb", None),
        check_vma=False,
    )
```

```python
import jax
import jax.numpy as jnp
from jax import lax
from jax.experimental import pallas as pl
from jax.experimental.pallas import tpu as pltpu
from jax.sharding import PartitionSpec as P

MESH = pl.DeviceIdType.MESH
STEPS = 16
TURNS = STEPS // 2
AHEAD = (4, 4, 5, 5, 10)
LAG = (1, 2, 2, 4, 5)
DIRECT = 2
PASS = 6


def stencil(cur, prev, nxt, z):
    row = lax.broadcasted_iota(jnp.int32, cur.shape, 0)
    n = cur.shape[1]
    near = pltpu.roll(jnp.where(row == 7, prev, cur), 1, 0) + pltpu.roll(jnp.where(row == 0, nxt, cur), 7, 0)
    far = pltpu.roll(jnp.where(row >= 6, prev, cur), 2, 0) + pltpu.roll(jnp.where(row <= 1, nxt, cur), 6, 0)
    near = near + (pltpu.roll(cur, 1, 1) + pltpu.roll(cur, n - 1, 1)) + (z[1] + z[2])
    far = far + (pltpu.roll(cur, 2, 1) + pltpu.roll(cur, n - 2, 1)) + (z[0] + z[3])
    return far * (1.0 / 120.0) - near * (2.0 / 15.0)


def kernel(
    coef, psi_hbm, pot_hbm, mine_hbm, zgot, psi, pot, first, h1, h2, term, got, zsend, mine, passing,
    load_sem, s1, r1, s2, r2, cs, cr, zs, zr, pass_in, pass_out,
):
    s, o = lax.axis_index("slab"), lax.axis_index("orb")
    count = lax.axis_size("slab")
    core, half = lax.rem(o, 2), o // 2
    up = {"slab": lax.rem(s + 1, count), "orb": o}
    down = {"slab": lax.rem(s + count - 1, count), "orb": o}
    mate = {"slab": s, "orb": o + 1 - 2 * core}
    far_chip = {"slab": s, "orb": lax.rem(o + 2, 4)}

    xy = lax.rem(s, 16)
    group = xy // 8
    turn = xy + group * (15 - 2 * xy)
    edge = s - xy + 15 * group

    def by(k, half_of=None):
        return {"slab": s - xy + k + group * (15 - 2 * k), "orb": o if half_of is None else half_of}

    barrier = pltpu.get_barrier_semaphore()

    @pl.when(turn == 0)
    def _():
        for k in range(1, TURNS):
            pl.semaphore_signal(barrier, inc=1, device_id=by(k, lax.rem(o + 2, 4)), device_id_type=MESH)

    @pl.when(turn != 0)
    def _():
        pl.semaphore_signal(barrier, inc=1, device_id={"slab": edge, "orb": o}, device_id_type=MESH)

    for who in (far_chip, up, down, mate):
        pl.semaphore_signal(barrier, inc=1, device_id=who, device_id_type=MESH)
    loads = [
        pltpu.make_async_copy(psi_hbm, psi, load_sem.at[0]),
        pltpu.make_async_copy(pot_hbm, pot, load_sem.at[1]),
    ]
    for copy in loads:
        copy.start()

    @pl.when(turn == 0)
    def _():
        pl.semaphore_wait(barrier, 4 + TURNS - 1)

    @pl.when(turn != 0)
    def _():
        pl.semaphore_wait(barrier, 5)

    def halo(src, dst, send, recv, k):
        return [
            pltpu.make_async_remote_copy(
                src_ref=src.at[pl.ds(2, 2), :, k],
                dst_ref=dst.at[0, :, :, k],
                send_sem=send.at[0, k],
                recv_sem=recv.at[0, k],
                device_id=up,
                device_id_type=MESH,
            ),
            pltpu.make_async_remote_copy(
                src_ref=src.at[pl.ds(0, 2), :, k],
                dst_ref=dst.at[1, :, :, k],
                send_sem=send.at[1, k],
                recv_sem=recv.at[1, k],
                device_id=down,
                device_id_type=MESH,
            ),
        ]

    def one(k):
        return halo(psi_hbm, h1, s1, r1, STEPS - 1 - k)

    def two(k):
        return halo(first, h2, s2, r2, STEPS - 1 - k)

    def to_mate(r):
        return pltpu.make_async_remote_copy(
            src_ref=term.at[1 - core, :, :, r],
            dst_ref=got.at[:, :, r],
            send_sem=cs.at[r],
            recv_sem=cr.at[r],
            device_id=mate,
            device_id_type=MESH,
        )

    def to_far(r):
        return pltpu.make_async_remote_copy(
            src_ref=zsend.at[:, r],
            dst_ref=zgot.at[:, r],
            send_sem=zs.at[r],
            recv_sem=zr.at[r],
            device_id=far_chip,
            device_id_type=MESH,
        )

    def to_pass(r, column):
        return pltpu.make_async_remote_copy(
            src_ref=zsend.at[:, r],
            dst_ref=passing,
            send_sem=zs.at[r],
            recv_sem=pass_in.at[0],
            device_id=by(column),
            device_id_type=MESH,
        )

    def start(copies):
        for copy in copies:
            copy.start()

    def received(copies):
        for copy in copies:
            copy.wait_recv()

    def tiles(own, halos, j, k):
        flat = j * STEPS + k
        before, after = lax.rem(flat + 2 * STEPS - 1, 2 * STEPS), lax.rem(flat + 1, 2 * STEPS)
        planes = [halos[0, 0, j, k], halos[0, 1, j, k]]
        planes += [own[p, j, k] for p in range(4)]
        planes += [halos[1, 0, j, k], halos[1, 1, j, k]]
        for p in range(4):
            prev = own[p, before // STEPS, lax.rem(before, STEPS)]
            nxt = own[p, after // STEPS, lax.rem(after, STEPS)]
            z = (planes[p], planes[p + 1], planes[p + 3], planes[p + 4])
            yield p, planes[p + 2], stencil(planes[p + 2], prev, nxt, z)

    def first_step(step):
        k = STEPS - 1 - step

        def body(j, carry):
            for p, cur, rest in tiles(psi, h1, j, k):
                first[p, j, k] = cur * (pot[p, j, k] * 0.2 - 0.05) + rest
            return carry

        lax.fori_loop(0, 2, body, 0)

    a = coef[0] - coef[2]
    b = coef[1]
    d = 2.0 * coef[2]

    def second_step(step):
        k = STEPS - 1 - step
        owner, r = k // TURNS, lax.rem(k, TURNS)

        def body(j, carry):
            for p, cur, rest in tiles(first, h2, j, k):
                scaled = cur * (pot[p, j, k] * 0.2 - 0.05) + rest
                value = a * psi[p, j, k] + b * cur + d * scaled
                term[owner, j, p, r] = value * value
            return carry

        lax.fori_loop(0, 2, body, 0)

        @pl.when(core != owner)
        def _():
            to_mate(r).start()

    def far_step(step):
        k = STEPS - 1 - step
        owner, r = k // TURNS, lax.rem(k, TURNS)

        @pl.when(core == owner)
        def _():
            to_mate(r).wait_recv()
            for p in range(4):
                zsend[p, r] = term[owner, 1 - half, p, r] + got[1 - half, p, r]
            column = lax.rem(r + core, TURNS)
            passes = jnp.logical_and(turn == 0, column >= DIRECT)

            @pl.when(passes)
            def _():
                to_pass(r, column).start()

            @pl.when(jnp.logical_not(passes))
            def _():
                to_far(r).start()

    def pass_on():
        to_pass(pass_row, turn).wait_recv()
        copy = pltpu.make_async_remote_copy(
            src_ref=passing,
            dst_ref=zgot.at[:, pass_row],
            send_sem=pass_out.at[0],
            recv_sem=zr.at[pass_row],
            device_id={"slab": edge, "orb": lax.rem(o + 2, 4)},
            device_id_type=MESH,
        )
        copy.start()
        copy.wait_send()

    def each(first_k, last_k, body):
        def step(k, carry):
            body(k)
            return carry

        lax.fori_loop(first_k, last_k, step, 0)

    def wraps(slab, width):
        return lax.rem(slab + width, count) // (2 * width) == 0

    def pick(table, slab):
        value = jnp.where(lax.rem(slab + 1, 4) // 2 == 0, table[1], table[0])
        value = jnp.where(lax.rem(slab + 1, 16) // 2 == 0, table[2], value)
        value = jnp.where(wraps(slab, 2), table[3], value)
        return jnp.where(wraps(slab, 1), table[4], value)

    ahead, lag = pick(AHEAD, s), pick(LAG, s)
    pass_row = lax.rem(turn - core + TURNS, TURNS)
    pass_slot = STEPS - 1 - core * TURNS - pass_row + pick(LAG, edge) + PASS

    each(0, ahead, lambda k: start(one(k)))
    for copy in loads:
        copy.wait()

    def slot(t):
        @pl.when(t < STEPS)
        def _():
            received(one(t))
            first_step(t)

            @pl.when(t > 0)
            def _():
                start(two(t))

            @pl.when(t + ahead < STEPS)
            def _():
                start(one(t + ahead))

            @pl.when(t == STEPS - 1)
            def _():
                start(two(0))

        m = t - lag

        @pl.when(jnp.logical_and(m > 1, m < STEPS + 2))
        def _():
            far_step(lax.rem(m - 1, STEPS))

        @pl.when(jnp.logical_and(m > 0, m < STEPS + 1))
        def _():
            k = lax.rem(m, STEPS)
            received(two(k))
            second_step(k)

        @pl.when(jnp.logical_and(t == pass_slot, turn >= DIRECT))
        def _():
            pass_on()

    each(0, STEPS + 2 + max(LAG) + PASS, slot)

    def own_sums(r):
        for p in range(4):
            mine[p, r] = term[core, half, p, r] + got[half, p, r]

    each(0, TURNS, own_sums)
    keep = pltpu.make_async_copy(mine, mine_hbm, load_sem.at[0])
    keep.start()
    each(0, TURNS, lambda r: to_far(r).wait_recv())
    keep.wait()

    def sent(k):
        for copy in (*one(k), *two(k)):
            copy.wait_send()

    each(0, STEPS, sent)

    def sums_sent(r):
        to_mate(r).wait_send()
        to_far(r).wait_send()

    each(0, TURNS, sums_sent)


def shards(orbitals, potential, coeffs):
    planes, rows, width = potential.shape
    grid = (planes, 2, STEPS, rows // (2 * STEPS), width)
    tile = grid[3:]
    halos = pltpu.VMEM((2, 2, 2, STEPS, *tile), jnp.float32)
    whole = pltpu.VMEM(grid, jnp.float32)
    quarter = (planes, TURNS, *tile)
    dma = pltpu.SemaphoreType.DMA
    mine, others = pl.pallas_call(
        kernel,
        out_shape=[jax.ShapeDtypeStruct(quarter, jnp.float32)] * 2,
        in_specs=[
            pl.BlockSpec(memory_space=pltpu.SMEM),
            pl.BlockSpec(memory_space=pl.ANY),
            pl.BlockSpec(memory_space=pl.ANY),
        ],
        out_specs=[pl.BlockSpec(memory_space=pl.ANY)] * 2,
        scratch_shapes=[
            whole, whole, whole, halos, halos,
            pltpu.VMEM((2, 2, *quarter), jnp.float32),
            pltpu.VMEM((2, *quarter), jnp.float32),
            pltpu.VMEM(quarter, jnp.float32),
            pltpu.VMEM(quarter, jnp.float32),
            pltpu.VMEM((planes, *tile), jnp.float32),
            dma((2,)),
            dma((2, STEPS)), dma((2, STEPS)), dma((2, STEPS)), dma((2, STEPS)),
            dma((TURNS,)), dma((TURNS,)), dma((TURNS,)), dma((TURNS,)), dma((1,)), dma((1,)),
        ],
        compiler_params=pltpu.CompilerParams(collective_id=0, has_side_effects=True),
        name="filter_density",
    )(coeffs, orbitals.reshape(grid), potential.reshape(grid))
    return ((mine + others) * 0.25).reshape(planes, rows // 4, width)


def solution(mesh):
    return jax.shard_map(
        shards,
        mesh=mesh,
        in_specs=(P("orb", "slab", None, None), P("slab", None, None), P()),
        out_specs=P("slab", "orb", None),
        check_vma=False,
    )
```

```python
import jax
import jax.numpy as jnp
from jax import lax
from jax.experimental import pallas as pl
from jax.experimental.pallas import tpu as pltpu
from jax.sharding import PartitionSpec as P

MESH = pl.DeviceIdType.MESH
STEPS = 16
TURNS = STEPS // 2
AHEAD = (4, 4, 5, 5, 10)
LAG = (1, 2, 2, 4, 5)
DIRECT = 2
PASS = 6


def stencil(cur, prev, nxt, z):
    row = lax.broadcasted_iota(jnp.int32, cur.shape, 0)
    n = cur.shape[1]
    near = pltpu.roll(jnp.where(row == 7, prev, cur), 1, 0) + pltpu.roll(jnp.where(row == 0, nxt, cur), 7, 0)
    far = pltpu.roll(jnp.where(row >= 6, prev, cur), 2, 0) + pltpu.roll(jnp.where(row <= 1, nxt, cur), 6, 0)
    near = near + (pltpu.roll(cur, 1, 1) + pltpu.roll(cur, n - 1, 1)) + (z[1] + z[2])
    far = far + (pltpu.roll(cur, 2, 1) + pltpu.roll(cur, n - 2, 1)) + (z[0] + z[3])
    return far * (1.0 / 120.0) - near * (2.0 / 15.0)


def kernel(
    coef, psi_hbm, pot_hbm, mine_hbm, zgot, psi, pot, first, h1, h2, term, got, zsend, mine, passing,
    load_sem, s1, r1, s2, r2, cs, cr, zs, zr, pass_in, pass_out,
):
    s, o = lax.axis_index("slab"), lax.axis_index("orb")
    count = lax.axis_size("slab")
    core, half = lax.rem(o, 2), o // 2
    up = {"slab": lax.rem(s + 1, count), "orb": o}
    down = {"slab": lax.rem(s + count - 1, count), "orb": o}
    mate = {"slab": s, "orb": o + 1 - 2 * core}
    far_chip = {"slab": s, "orb": lax.rem(o + 2, 4)}

    xy = lax.rem(s, 16)
    group = xy // 8
    turn = xy + group * (15 - 2 * xy)
    edge = s - xy + 15 * group

    def by(k, half_of=None):
        return {"slab": s - xy + k + group * (15 - 2 * k), "orb": o if half_of is None else half_of}

    barrier = pltpu.get_barrier_semaphore()

    @pl.when(turn == 0)
    def _():
        for k in range(1, TURNS):
            pl.semaphore_signal(barrier, inc=1, device_id=by(k, lax.rem(o + 2, 4)), device_id_type=MESH)

    @pl.when(turn != 0)
    def _():
        pl.semaphore_signal(barrier, inc=1, device_id={"slab": edge, "orb": o}, device_id_type=MESH)

    for who in (far_chip, up, down, mate):
        pl.semaphore_signal(barrier, inc=1, device_id=who, device_id_type=MESH)
    loads = [
        pltpu.make_async_copy(psi_hbm, psi, load_sem.at[0]),
        pltpu.make_async_copy(pot_hbm, pot, load_sem.at[1]),
    ]
    for copy in loads:
        copy.start()

    @pl.when(turn == 0)
    def _():
        pl.semaphore_wait(barrier, 4 + TURNS - 1)

    @pl.when(turn != 0)
    def _():
        pl.semaphore_wait(barrier, 5)

    def halo(src, dst, send, recv, k):
        return [
            pltpu.make_async_remote_copy(
                src_ref=src.at[pl.ds(2, 2), :, k],
                dst_ref=dst.at[0, :, :, k],
                send_sem=send.at[0, k],
                recv_sem=recv.at[0, k],
                device_id=up,
                device_id_type=MESH,
            ),
            pltpu.make_async_remote_copy(
                src_ref=src.at[pl.ds(0, 2), :, k],
                dst_ref=dst.at[1, :, :, k],
                send_sem=send.at[1, k],
                recv_sem=recv.at[1, k],
                device_id=down,
                device_id_type=MESH,
            ),
        ]

    def one(k):
        return halo(psi_hbm, h1, s1, r1, STEPS - 1 - k)

    def two(k):
        return halo(first, h2, s2, r2, STEPS - 1 - k)

    def to_mate(r):
        return pltpu.make_async_remote_copy(
            src_ref=term.at[1 - core, :, :, r],
            dst_ref=got.at[:, :, r],
            send_sem=cs.at[r],
            recv_sem=cr.at[r],
            device_id=mate,
            device_id_type=MESH,
        )

    def to_far(r):
        return pltpu.make_async_remote_copy(
            src_ref=zsend.at[:, r],
            dst_ref=zgot.at[:, r],
            send_sem=zs.at[r],
            recv_sem=zr.at[r],
            device_id=far_chip,
            device_id_type=MESH,
        )

    def to_pass(r, column):
        return pltpu.make_async_remote_copy(
            src_ref=zsend.at[:, r],
            dst_ref=passing,
            send_sem=zs.at[r],
            recv_sem=pass_in.at[0],
            device_id=by(column),
            device_id_type=MESH,
        )

    def start(copies):
        for copy in copies:
            copy.start()

    def received(copies):
        for copy in copies:
            copy.wait_recv()

    def tiles(own, halos, j, k):
        flat = j * STEPS + k
        before, after = lax.rem(flat + 2 * STEPS - 1, 2 * STEPS), lax.rem(flat + 1, 2 * STEPS)
        planes = [halos[0, 0, j, k], halos[0, 1, j, k]]
        planes += [own[p, j, k] for p in range(4)]
        planes += [halos[1, 0, j, k], halos[1, 1, j, k]]
        for p in range(4):
            prev = own[p, before // STEPS, lax.rem(before, STEPS)]
            nxt = own[p, after // STEPS, lax.rem(after, STEPS)]
            z = (planes[p], planes[p + 1], planes[p + 3], planes[p + 4])
            yield p, planes[p + 2], stencil(planes[p + 2], prev, nxt, z)

    def first_step(step):
        k = STEPS - 1 - step

        def body(j, carry):
            for p, cur, rest in tiles(psi, h1, j, k):
                first[p, j, k] = cur * (pot[p, j, k] * 0.2 - 0.05) + rest
            return carry

        lax.fori_loop(0, 2, body, 0)

    a = coef[0] - coef[2]
    b = coef[1]
    d = 2.0 * coef[2]

    def second_step(step):
        k = STEPS - 1 - step
        owner, r = k // TURNS, lax.rem(k, TURNS)

        def body(j, carry):
            for p, cur, rest in tiles(first, h2, j, k):
                scaled = cur * (pot[p, j, k] * 0.2 - 0.05) + rest
                value = a * psi[p, j, k] + b * cur + d * scaled
                term[owner, j, p, r] = value * value
            return carry

        lax.fori_loop(0, 2, body, 0)

        @pl.when(core != owner)
        def _():
            to_mate(r).start()

    def far_step(step):
        k = STEPS - 1 - step
        owner, r = k // TURNS, lax.rem(k, TURNS)

        @pl.when(core == owner)
        def _():
            to_mate(r).wait_recv()
            for p in range(4):
                zsend[p, r] = term[owner, 1 - half, p, r] + got[1 - half, p, r]
            column = lax.rem(r + core, TURNS)
            passes = jnp.logical_and(turn == 0, column >= DIRECT)

            @pl.when(passes)
            def _():
                to_pass(r, column).start()

            @pl.when(jnp.logical_not(passes))
            def _():
                to_far(r).start()

    def passed():
        return pltpu.make_async_remote_copy(
            src_ref=passing,
            dst_ref=zgot.at[:, pass_row],
            send_sem=pass_out.at[0],
            recv_sem=zr.at[pass_row],
            device_id={"slab": edge, "orb": lax.rem(o + 2, 4)},
            device_id_type=MESH,
        )

    def pass_on():
        to_pass(pass_row, turn).wait_recv()
        passed().start()

    def each(first_k, last_k, body):
        def step(k, carry):
            body(k)
            return carry

        lax.fori_loop(first_k, last_k, step, 0)

    def wraps(slab, width):
        return lax.rem(slab + width, count) // (2 * width) == 0

    def pick(table, slab):
        value = jnp.where(lax.rem(slab + 1, 4) // 2 == 0, table[1], table[0])
        value = jnp.where(lax.rem(slab + 1, 16) // 2 == 0, table[2], value)
        value = jnp.where(wraps(slab, 2), table[3], value)
        return jnp.where(wraps(slab, 1), table[4], value)

    ahead, lag = pick(AHEAD, s), pick(LAG, s)
    pass_row = lax.rem(turn - core + TURNS, TURNS)
    pass_slot = STEPS - 1 - core * TURNS - pass_row + pick(LAG, edge) + PASS

    each(0, ahead, lambda k: start(one(k)))
    for copy in loads:
        copy.wait()

    def slot(t):
        @pl.when(t < STEPS)
        def _():
            received(one(t))
            first_step(t)

            @pl.when(t > 0)
            def _():
                start(two(t))

            @pl.when(t + ahead < STEPS)
            def _():
                start(one(t + ahead))

            @pl.when(t == STEPS - 1)
            def _():
                start(two(0))

        m = t - lag

        @pl.when(jnp.logical_and(m > 1, m < STEPS + 2))
        def _():
            far_step(lax.rem(m - 1, STEPS))

        @pl.when(jnp.logical_and(m > 0, m < STEPS + 1))
        def _():
            k = lax.rem(m, STEPS)
            received(two(k))
            second_step(k)

        @pl.when(jnp.logical_and(t == pass_slot, turn >= DIRECT))
        def _():
            pass_on()

    each(0, STEPS + 2 + max(LAG) + PASS, slot)

    def own_sums(r):
        for p in range(4):
            mine[p, r] = term[core, half, p, r] + got[half, p, r]

    each(0, TURNS, own_sums)
    keep = pltpu.make_async_copy(mine, mine_hbm, load_sem.at[0])
    keep.start()
    each(0, TURNS, lambda r: to_far(r).wait_recv())
    keep.wait()

    def sent(k):
        for copy in (*one(k), *two(k)):
            copy.wait_send()

    each(0, STEPS, sent)

    def sums_sent(r):
        to_mate(r).wait_send()
        to_far(r).wait_send()

    each(0, TURNS, sums_sent)

    @pl.when(turn >= DIRECT)
    def _():
        passed().wait_send()


def shards(orbitals, potential, coeffs):
    planes, rows, width = potential.shape
    grid = (planes, 2, STEPS, rows // (2 * STEPS), width)
    tile = grid[3:]
    halos = pltpu.VMEM((2, 2, 2, STEPS, *tile), jnp.float32)
    whole = pltpu.VMEM(grid, jnp.float32)
    quarter = (planes, TURNS, *tile)
    dma = pltpu.SemaphoreType.DMA
    mine, others = pl.pallas_call(
        kernel,
        out_shape=[jax.ShapeDtypeStruct(quarter, jnp.float32)] * 2,
        in_specs=[
            pl.BlockSpec(memory_space=pltpu.SMEM),
            pl.BlockSpec(memory_space=pl.ANY),
            pl.BlockSpec(memory_space=pl.ANY),
        ],
        out_specs=[pl.BlockSpec(memory_space=pl.ANY)] * 2,
        scratch_shapes=[
            whole, whole, whole, halos, halos,
            pltpu.VMEM((2, 2, *quarter), jnp.float32),
            pltpu.VMEM((2, *quarter), jnp.float32),
            pltpu.VMEM(quarter, jnp.float32),
            pltpu.VMEM(quarter, jnp.float32),
            pltpu.VMEM((planes, *tile), jnp.float32),
            dma((2,)),
            dma((2, STEPS)), dma((2, STEPS)), dma((2, STEPS)), dma((2, STEPS)),
            dma((TURNS,)), dma((TURNS,)), dma((TURNS,)), dma((TURNS,)), dma((1,)), dma((1,)),
        ],
        compiler_params=pltpu.CompilerParams(collective_id=0, has_side_effects=True),
        name="filter_density",
    )(coeffs, orbitals.reshape(grid), potential.reshape(grid))
    return ((mine + others) * 0.25).reshape(planes, rows // 4, width)


def solution(mesh):
    return jax.shard_map(
        shards,
        mesh=mesh,
        in_specs=(P("orb", "slab", None, None), P("slab", None, None), P()),
        out_specs=P("slab", "orb", None),
        check_vma=False,
    )
```
